1024 devices in a mesh: sub: 256 (over y, z, core), grp: 4 (over x).
Axes of the slice: x: 4, y: 4, z: 32, core: 2. Of those that a mesh axis runs over, the one named last changes fastest.
Arguments:
- dual_ops: float32 [256, 4, 576, 576], P('sub', 'grp'), as said below
- gap_parts: float32 [256, 4, 576, 256], P('sub', 'grp')
- modes: float32 [256, 4, 576, 48], P('sub', 'grp'), may hold values from -0.25 to 0.25
- coarse_rows: float32 [256, 4, 48, 192], P('sub', 'grp'), as said below
- face_live: int32 [256, 4, 6], P('sub', 'grp'), may hold values from 0 to 1, as said below
- contact: int32 [256, 4, 6], P('sub', 'grp'), may hold values from 0 to 1, as said below
Outputs:
- multipliers: float32 [256, 4, 576, 256], P('sub', 'grp')
- direction: float32 [256, 4, 576, 256], P('sub', 'grp')
The draws below stay inside these ranges and needn't reach their ends.
Inputs may be any that keep to these rules, and one draw needn't show every extreme that they name: Slot k of face_live is 1 only where the subdomain across slot k exists in the geometry (slots 0 and 1 stay within one row of 16 subdomains along sub), and it equals the flag of slot k XOR 1 of that subdomain; face blocks across a shared face list the same points in the same order. `contact`: 1 only where face_live is 1, and equal on both sides of a face. `dual_ops`: each subdomain's block is symmetric positive definite. `coarse_rows`: for each index along sub, the rows of the 4 subdomains stacked in grp order form a symmetric matrix.
All inputs are finite; a program needn't handle non-finite values.
Results may differ from the reference program's by a relative error of at most 0.00012.
Values sent between devices are 32-bit elements; how exact they have to be, the bound alone decides.
No kernel may reach another device: no remote copies, remote signals or barrier semaphores. Data moves between devices by JAX's collectives and lax.ppermute only.
A program may use at most 32 MiB of HBM per device.

```python
import math
import jax
import jax.numpy as jnp
from jax import lax

FACE = 96
MODES = 48
SUBROW = 16
CASES = 256
ITERS = 2
DUAL = 576
SUBS = 256
GROUPS = 4


def draw_dual_ops(key, part):
    noise = jax.random.normal(key, (SUBS, GROUPS, DUAL, DUAL), jnp.float32)
    symmetric = (noise + jnp.swapaxes(noise, 2, 3)) * 0.5 ** 0.5 / DUAL ** 0.5
    diagonal_part = jnp.exp(jax.random.uniform(jax.random.fold_in(key, 7), (SUBS, GROUPS, DUAL, 1), jnp.float32, math.log(3.0), math.log(12.0)))
    identity = jnp.eye(DUAL, dtype=jnp.float32)[None, None]
    return symmetric + identity * diagonal_part


def draw_gap_parts(key, part):
    values = jax.random.normal(key, (SUBS, GROUPS, DUAL, CASES), jnp.float32)
    ramp = 3.0 ** (jnp.arange(SUBS, dtype=jnp.float32) / max(SUBS - 1, 1))
    return values * ramp[:, None, None, None]


def draw_coarse_rows(key, part):
    width = GROUPS * MODES
    noise = jax.random.normal(key, (SUBS, width, width), jnp.float32)
    symmetric = (noise + jnp.swapaxes(noise, 1, 2)) * 0.5 ** 0.5 * 0.25 / width ** 0.5
    whole = symmetric + 0.7 * jnp.eye(width, dtype=jnp.float32)[None]
    return whole.reshape(SUBS, GROUPS, MODES, width)


def shift_down(edges, axis, offset):
    rolled = jnp.roll(edges, offset, axis=axis)
    places = jnp.arange(edges.shape[axis])
    keep = (places >= offset).astype(jnp.int32)
    if axis == 0:
        return rolled * keep[:, None]
    return rolled * keep[None, :]


def face_flags(key):
    position = jnp.broadcast_to(jnp.arange(SUBS)[:, None], (SUBS, GROUPS))
    group_pos = jnp.broadcast_to(jnp.arange(GROUPS)[None, :], (SUBS, GROUPS))
    valid = jnp.stack([((position + 1) % SUBROW != 0) & (position + 1 < SUBS), position + SUBROW < SUBS, group_pos + 1 < GROUPS]).astype(jnp.int32)
    linked = (jax.random.randint(jax.random.fold_in(key, 11), (3, SUBS, GROUPS), 0, 4) > 0).astype(jnp.int32) * valid
    touching = jax.random.randint(jax.random.fold_in(key, 13), (3, SUBS, GROUPS), 0, 2) * linked
    return (linked, touching)


def spread_slots(edges):
    return jnp.stack([shift_down(edges[0], 0, 1), edges[0], shift_down(edges[1], 0, SUBROW), edges[1], shift_down(edges[2], 1, 1), edges[2]], axis=-1).astype(jnp.int32)


def draw_face_live(key, part):
    linked, touching = face_flags(key)
    return spread_slots(linked)


def draw_contact(key, part):
    linked, touching = face_flags(key)
    return spread_slots(touching)


def block_levels(own_key, shape, shards, low, high):
    def one(axis_at, blocks):
        steps = jax.random.uniform(jax.random.fold_in(jax.random.fold_in(own_key, 6), axis_at), (blocks,), jnp.float32, low / len(shards), high / len(shards))
        return jnp.repeat(jnp.exp(steps), shape[axis_at] // blocks).reshape((-1,) + (1,) * (len(shape) - axis_at - 1))

    loudness = one(*shards[0])
    for cut in shards[1:]:
        loudness = loudness * one(*cut)
    return loudness


def bell_draw(own_key, extent, scale, bound, pieces=(), kind=jnp.bfloat16):
    drawn = jax.random.normal(own_key, extent, jnp.float32) * scale
    if len(pieces) > 0:
        drawn = block_levels(own_key, extent, pieces, -0.22, 0.18) * drawn
    return jnp.clip(drawn, min=-bound, max=bound).astype(kind)


def setup_inputs(seed: int = 0) -> dict:
    seeds = jax.random.split(jax.random.key(seed), 7)
    dual_ops = draw_dual_ops(jax.random.fold_in(seeds[6], 71), 0)
    gap_parts = draw_gap_parts(jax.random.fold_in(seeds[6], 71), 0)
    modes = bell_draw(seeds[2], (SUBS, GROUPS, DUAL, MODES), DUAL ** -0.5, 0.25, ((0, 256), (1, 4)), jnp.float32)
    coarse_rows = draw_coarse_rows(jax.random.fold_in(seeds[6], 71), 0)
    face_live = draw_face_live(jax.random.fold_in(seeds[6], 71), 0)
    contact = draw_contact(jax.random.fold_in(seeds[6], 71), 0)
    return {"dual_ops": dual_ops, "gap_parts": gap_parts, "modes": modes, "coarse_rows": coarse_rows, "face_live": face_live, "contact": contact}


def lower(values, axis, offset):
    count = values.shape[axis]
    if offset == 0:
        return values
    if abs(offset) >= count:
        return jnp.zeros_like(values)
    widths = [(0, 0)] * values.ndim
    if offset > 0:
        widths[axis] = (offset, 0)
        padded = jnp.pad(values, widths)
        return lax.slice_in_dim(padded, 0, count, axis=axis)
    widths[axis] = (0, -offset)
    padded = jnp.pad(values, widths)
    return lax.slice_in_dim(padded, -offset, -offset + count, axis=axis)


def across(view):
    return jnp.stack([lower(view[:, :, 1], 0, 1), lower(view[:, :, 0], 0, -1),
                      lower(view[:, :, 3], 0, SUBROW), lower(view[:, :, 2], 0, -SUBROW),
                      lower(view[:, :, 5], 1, 1), lower(view[:, :, 4], 1, -1)], axis=2)


def assemble(values, live_view):
    view = values.reshape(SUBS, GROUPS, 6, FACE, values.shape[-1])
    return (live_view * (view - across(view))).reshape(values.shape)


def apply_ops(dual_ops, values, live_view):
    products = jnp.einsum('sgij,sgjl->sgil', dual_ops, values, precision=lax.Precision.HIGHEST)
    return assemble(products, live_view)


def slot_rows(flags):
    spread = jnp.broadcast_to(flags[:, :, :, None, None], (SUBS, GROUPS, 6, FACE, 1))
    return spread.reshape(SUBS, GROUPS, DUAL, 1)


def reference(dual_ops, gap_parts, modes, coarse_rows, face_live, contact):
    highest = lax.Precision.HIGHEST
    live_view = face_live.astype(jnp.float32)[:, :, :, None, None]
    live_rows = slot_rows(face_live.astype(jnp.float32))
    parity = (jnp.arange(6) % 2).astype(jnp.int32)[None, None, :]
    upper_rows = slot_rows(contact * parity) > 0
    lower_rows = slot_rows(contact * (1 - parity)) > 0
    masked = modes * live_rows
    gap = assemble(gap_parts, live_view)
    blocks = coarse_rows.reshape(SUBS, GROUPS, MODES, GROUPS, MODES)
    multipliers = jnp.zeros((SUBS, GROUPS, DUAL, CASES), jnp.float32)
    direction = multipliers
    for turn in range(ITERS):
        gradient = apply_ops(dual_ops, multipliers, live_view) - gap
        coef = jnp.einsum('sgdm,sgdl->sgml', masked, gradient, precision=highest)
        coarse = jnp.einsum('sgmhn,shnl->sgml', blocks, coef, precision=highest)
        correction = assemble(jnp.einsum('sgdm,sgml->sgdl', masked, coarse, precision=highest), live_view)
        direction = gradient - correction
        image = apply_ops(dual_ops, direction, live_view)
        norm = jnp.sum(direction * direction, axis=(0, 1, 2))
        curvature = jnp.sum(direction * image, axis=(0, 1, 2))
        trial = multipliers - (norm / curvature) * direction
        multipliers = jnp.where(upper_rows, jnp.maximum(trial, 0.0),
                                jnp.where(lower_rows, jnp.minimum(trial, 0.0), trial))
    return multipliers, direction
```

```python
import jax
import jax.numpy as jnp
from jax import lax
from jax.sharding import PartitionSpec as P

SUBROW = 16
SOURCES = (("sub", -1), ("sub", 1), ("sub", -SUBROW), ("sub", SUBROW), ("grp", -1), ("grp", 1))
ORDER = (2, 3, 0, 1, 4, 5)


def shifted(array, axis, by):
    count = lax.axis_size(axis)
    pairs = [(i, i + by) for i in range(count) if 0 <= i + by < count]
    return lax.ppermute(array, axis, pairs)


def fetch(piece, slot):
    axis, offset = SOURCES[slot]
    return shifted(piece, axis, -offset)


def across(view):
    gotten = [None] * 6
    for slot in ORDER:
        gotten[slot] = fetch(view[slot ^ 1], slot)
    return jnp.stack(gotten)


def matmul(left, right):
    return jnp.dot(left, right, precision=lax.Precision.HIGHEST, preferred_element_type=jnp.float32)


def clamp(values, upper, lower):
    return jnp.where(upper, jnp.maximum(values, 0.0), jnp.where(lower, jnp.minimum(values, 0.0), values))


def total(terms):
    return lax.psum(terms, ("sub", "grp"))


def body(dual_ops, gap_parts, modes, coarse_rows, face_live, contact):
    operator = dual_ops[0, 0]
    dual_rows = operator.shape[0]
    face_rows = dual_rows // 6
    cases = gap_parts.shape[3]
    kinds = modes.shape[3]
    live_flags = face_live[0, 0].astype(jnp.float32)
    live_view = live_flags[:, None, None]
    parity = jnp.arange(6) % 2
    upper = (contact[0, 0] * parity)[:, None, None] > 0
    lower = (contact[0, 0] * (1 - parity))[:, None, None] > 0
    masked = modes[0, 0].reshape(6, face_rows, kinds) * live_view
    own_rows = coarse_rows[0, 0]

    parts = gap_parts[0, 0].reshape(6, face_rows, cases)
    parts_across = across(parts)
    masked_across = across(masked)
    all_rows = jnp.concatenate([own_rows, fetch(own_rows, 4), fetch(own_rows, 5)])

    masked_flat = masked.reshape(dual_rows, kinds)
    pairs = jnp.concatenate([masked, -masked_across], axis=2)

    def projected(values):
        coef = matmul(masked_flat.T, values.reshape(dual_rows, cases))
        coarse = matmul(all_rows, lax.all_gather(coef, "grp", axis=0, tiled=True))
        own = coarse[:kinds]
        near = [None] * 4
        for slot in ORDER[:4]:
            near[slot] = fetch(own, slot)
        near += [coarse[kinds:2 * kinds], coarse[2 * kinds:]]
        stacked = jnp.stack([jnp.concatenate([own, other]) for other in near])
        correction = jnp.einsum(
            "kij,kjl->kil", pairs, stacked, precision=lax.Precision.HIGHEST, preferred_element_type=jnp.float32
        )
        return values - correction

    def apply_local(values):
        return matmul(operator, values.reshape(dual_rows, cases)).reshape(6, face_rows, cases)

    first = projected(live_view * (parts_across - parts))
    push = clamp(-first, upper, lower)
    pushed = apply_local(push)
    first_image = apply_local(first)
    change = projected(live_view * (pushed - across(pushed)))
    change_image = apply_local(change)

    def inner(left, right):
        return jnp.sum(left * right, axis=(0, 1))

    sums = total(jnp.stack([
        inner(first, first), inner(first, first_image), inner(first, change),
        inner(change, change), inner(change, first_image), inner(change, change_image),
    ]))
    step = sums[0] / (2.0 * sums[1])
    norm = sums[0] + step * (2.0 * sums[2] + step * sums[3])
    curvature = 2.0 * (sums[1] + step * (2.0 * sums[4] + step * sums[5]))
    direction = first + step * change
    multipliers = clamp(step * push - (norm / curvature) * direction, upper, lower)
    shape = (1, 1, dual_rows, cases)
    return (multipliers.reshape(shape), direction.reshape(shape))


def solution(mesh):
    in_specs = (
        P("sub", "grp", None, None),
        P("sub", "grp", None, None),
        P("sub", "grp", None, None),
        P("sub", "grp", None, None),
        P("sub", "grp", None),
        P("sub", "grp", None),
    )
    out_specs = (P("sub", "grp", None, None), P("sub", "grp", None, None))
    return jax.shard_map(body, mesh=mesh, in_specs=in_specs, out_specs=out_specs, check_vma=False)
```

```python
import jax
import jax.numpy as jnp
from jax import lax
from jax.sharding import Mesh, PartitionSpec as P


SUBROW = 16
PLANE = ("y", "core", "grp")
SUB = ("y", "z", "core")
SOURCES = ((SUB, -1), (SUB, 1), (SUB, -SUBROW), (SUB, SUBROW), ("grp", -1), ("grp", 1))
ORDER = (2, 3, 0, 1, 4, 5)


def fetch(piece, slot):
    axis, offset = SOURCES[slot]
    count = lax.axis_size(axis)
    pairs = [(i, i - offset) for i in range(count) if 0 <= i - offset < count]
    return lax.ppermute(piece, axis, pairs)


def exchange(pieces):
    gotten = [None] * len(pieces)
    for slot in ORDER:
        if slot < len(pieces):
            gotten[slot] = fetch(pieces[slot], slot)
    return gotten


def matmul(left, right):
    return jnp.dot(left, right, precision=lax.Precision.HIGHEST, preferred_element_type=jnp.float32)


def clamp(values, upper, lower):
    return jnp.where(upper, jnp.maximum(values, 0.0), jnp.where(lower, jnp.minimum(values, 0.0), values))


def swap(blocks, axes):
    return lax.all_to_all(blocks, axes, 0, 0, tiled=True)


def total(terms):
    plane = lax.axis_size(PLANE)
    chunks = terms.reshape(plane, -1)
    chunk = jnp.sum(swap(chunks, PLANE), axis=0)
    chunk = jnp.sum(swap(jnp.broadcast_to(chunk, (lax.axis_size("z"),) + chunk.shape), "z"), axis=0)
    return swap(jnp.broadcast_to(chunk, chunks.shape), PLANE).reshape(terms.shape)


def gather(block):
    count = lax.axis_size("grp")
    return swap(jnp.broadcast_to(block, (count,) + block.shape), "grp").reshape(-1, block.shape[-1])


def body(dual_ops, gap_parts, modes, coarse_rows, face_live, contact):
    operator = dual_ops[0, 0]
    dual_rows = operator.shape[0]
    face_rows = dual_rows // 6
    cases = gap_parts.shape[3]
    kinds = modes.shape[3]
    half = kinds // 2
    lanes = cases // 2
    live_flags = face_live[0, 0].astype(jnp.float32)
    live_view = live_flags[:, None, None]
    parity = jnp.arange(6) % 2
    upper = (contact[0, 0] * parity)[:, None, None] > 0
    lower = (contact[0, 0] * (1 - parity))[:, None, None] > 0
    own_rows = coarse_rows[0, 0]
    parts = gap_parts[0, 0].reshape(6, face_rows, cases)
    shapes = modes[0, 0].T.reshape(kinds, 6, face_rows)

    messages = []
    for slot in range(6):
        wide = jnp.pad(shapes[:, slot ^ 1], ((0, 0), (0, lanes - face_rows)))
        message = [parts[slot ^ 1], jnp.concatenate([wide[:half], wide[half:]], axis=1)]
        if slot >= 4:
            message.append(jnp.pad(own_rows, ((0, 0), (0, cases - own_rows.shape[1]))))
        messages.append(jnp.concatenate(message))
    gotten = exchange(messages)
    parts_across = jnp.stack([message[:face_rows] for message in gotten])
    pairs = []
    for slot in range(6):
        packed = gotten[slot][face_rows:face_rows + half]
        other = jnp.concatenate([packed[:, :face_rows], packed[:, lanes:lanes + face_rows]])
        pairs.append(live_flags[slot] * jnp.concatenate([shapes[:, slot], -other]))
    pairs = jnp.stack(pairs)
    masked = jnp.repeat(live_flags, face_rows)[None, :] * shapes.reshape(kinds, dual_rows)
    near_rows = [gotten[slot][face_rows + half:, :own_rows.shape[1]] for slot in (4, 5)]
    all_rows = jnp.concatenate([own_rows] + near_rows)

    def projected(values):
        coef = matmul(masked, values.reshape(dual_rows, cases))
        coarse = matmul(all_rows, gather(coef))
        own = coarse[:kinds]
        near = exchange([own] * 4) + [coarse[kinds:2 * kinds], coarse[2 * kinds:]]
        stacked = jnp.stack([jnp.concatenate([own, other]) for other in near])
        correction = jnp.einsum(
            "kmi,kml->kil", pairs, stacked, precision=lax.Precision.HIGHEST, preferred_element_type=jnp.float32
        )
        return values - correction

    def apply_local(values):
        return matmul(operator, values.reshape(dual_rows, cases)).reshape(6, face_rows, cases)

    first = projected(live_view * (parts_across - parts))
    push = clamp(-first, upper, lower)
    pushed = apply_local(push)
    first_image = apply_local(first)
    pushed_across = jnp.stack(exchange([pushed[slot ^ 1] for slot in range(6)]))
    change = projected(live_view * (pushed - pushed_across))
    change_image = apply_local(change)

    def inner(left, right):
        return jnp.sum(left * right, axis=(0, 1))

    sums = total(jnp.stack([
        inner(first, first), inner(first, first_image), inner(first, change),
        inner(change, change), inner(change, first_image), inner(change, change_image),
    ]))
    step = sums[0] / (2.0 * sums[1])
    norm = sums[0] + step * (2.0 * sums[2] + step * sums[3])
    curvature = 2.0 * (sums[1] + step * (2.0 * sums[4] + step * sums[5]))
    direction = first + step * change
    multipliers = clamp(step * push - (norm / curvature) * direction, upper, lower)
    shape = (1, 1, dual_rows, cases)
    return (multipliers.reshape(shape), direction.reshape(shape))


def solution(mesh):
    fine = Mesh(mesh.devices.reshape(4, 32, 2, 4), ("y", "z", "core", "grp"))
    wide = P(SUB, "grp", None, None)
    flags = P(SUB, "grp", None)
    return jax.shard_map(
        body, mesh=fine, in_specs=(wide, wide, wide, wide, flags, flags), out_specs=(wide, wide), check_vma=False
    )
```

```python
import functools

import jax
import jax.numpy as jnp
from jax import lax
from jax.experimental import pallas as pl
from jax.experimental.pallas import tpu as pltpu
from jax.sharding import Mesh, PartitionSpec as P


SUBROW = 16
SLOTS = 6
LANES = 128
PLANE = ("y", "core", "grp")
SUB = ("y", "z", "core")
SOURCES = ((SUB, -1), (SUB, 1), (SUB, -SUBROW), (SUB, SUBROW), ("grp", -1), ("grp", 1))
ORDER = (2, 3, 0, 1, 4, 5)


def fetch(piece, slot):
    axis, offset = SOURCES[slot]
    count = lax.axis_size(axis)
    pairs = [(i, i - offset) for i in range(count) if 0 <= i - offset < count]
    return lax.ppermute(piece, axis, pairs)


def exchange(pieces):
    gotten = [None] * len(pieces)
    for slot in ORDER:
        if slot < len(pieces):
            gotten[slot] = fetch(pieces[slot], slot)
    return gotten


def swap(blocks, axes):
    return lax.all_to_all(blocks, axes, 0, 0, tiled=True)


def total(terms):
    plane = lax.axis_size(PLANE)
    chunks = terms.reshape(plane, -1)
    chunk = jnp.sum(swap(chunks, PLANE), axis=0)
    chunk = jnp.sum(swap(jnp.broadcast_to(chunk, (lax.axis_size("z"),) + chunk.shape), "z"), axis=0)
    return swap(jnp.broadcast_to(chunk, chunks.shape), PLANE).reshape(terms.shape)


def dot(left, right, across=1):
    return lax.dot_general(
        left, right, (((across,), (0,)), ((), ())),
        precision=lax.Precision.HIGHEST, preferred_element_type=jnp.float32,
    )


def clamp(values, slot, touching):
    bounded = jnp.maximum(values, 0.0) if slot % 2 else jnp.minimum(values, 0.0)
    return jnp.where(touching, bounded, values)


def kernel_call(body, flags, arrays, outs, flops):
    smem = pl.BlockSpec(memory_space=pltpu.SMEM)
    vmem = pl.BlockSpec(memory_space=pltpu.VMEM)
    moved = sum(a.size for a in arrays) + sum(o[0] * o[1] if len(o) == 2 else o[0] * o[1] * o[2] for o in outs)
    return pl.pallas_call(
        functools.partial(body, len(flags), len(arrays)),
        out_shape=[jax.ShapeDtypeStruct(o, jnp.float32) for o in outs],
        in_specs=[smem] * len(flags) + [vmem] * len(arrays),
        out_specs=[vmem] * len(outs),
        compiler_params=pltpu.CompilerParams(vmem_limit_bytes=24 << 20),
        cost_estimate=pl.CostEstimate(flops=flops, bytes_accessed=4 * moved, transcendentals=0),
    )(*flags, *arrays)


def split(refs, flags, arrays):
    return refs[:flags], refs[flags:flags + arrays], refs[flags + arrays:]


def pack_kernel(nf, na, *refs):
    _, (gap, shapes, rows), outs = split(refs, nf, na)
    face = gap.shape[0] // SLOTS
    half = shapes.shape[0] // 2
    for slot, out in enumerate(outs):
        at = (slot ^ 1) * face
        out[:face] = gap[at:at + face]
        piece = shapes[:, at:at + face]
        out[face:face + half] = jnp.zeros((half, out.shape[1]), jnp.float32)
        out[face:face + half, :face] = piece[:half]
        out[face:face + half, LANES:LANES + face] = piece[half:]
        if slot >= 4:
            out[face + half:] = jnp.zeros((2 * half, out.shape[1]), jnp.float32)
            out[face + half:, :rows.shape[1]] = rows[...]


def residual_kernel(sign, nf, na, *refs):
    (live,), (own, shapes, *gotten), (values, spread) = split(refs, nf, na)
    face = values.shape[0] // SLOTS
    for slot in range(SLOTS):
        at = slot * face
        gap = own[at:at + face] if own.shape[0] == values.shape[0] else None
        values[at:at + face] = live[0, slot].astype(jnp.float32) * (sign * (gap - gotten[slot][:face]))
    coef = dot(shapes[...], values[...])
    for row in range(spread.shape[0]):
        spread[row] = coef


def coarse_kernel(nf, na, *refs):
    _, (rows, coefs), (own,) = split(refs, nf, na)
    own[...] = dot(rows[...], coefs[...])


def corrected(live, values, shapes, own, coefs, near, messages):
    face = values.shape[0] // SLOTS
    kinds = shapes.shape[0]
    half = kinds // 2
    mine = dot(shapes[...].T, own[...])
    faces = []
    for slot in range(SLOTS):
        at = slot * face
        message = messages[slot]
        if slot < 4:
            other = near[slot][...]
        else:
            other = dot(message[face + half:, :coefs.shape[0]], coefs[...])
        packed = message[face:face + half]
        theirs = dot(jnp.concatenate([packed[:, :face], packed[:, LANES:LANES + face]]).T, other)
        keep = live[0, slot].astype(jnp.float32)
        faces.append(values[at:at + face] - keep * (mine[at:at + face] - theirs))
    return faces


def push_kernel(nf, na, *refs):
    (live, contact), (values, operator, shapes, own, coefs, *rest), (first, push, *pushed) = split(refs, nf, na)
    near, messages = rest[:4], rest[4:]
    face = values.shape[0] // SLOTS
    for slot, part in enumerate(corrected(live, values, shapes, own, coefs, near, messages)):
        at = slot * face
        first[at:at + face] = part
        push[at:at + face] = clamp(-part, slot, contact[0, slot] > 0)
    for slot in range(SLOTS):
        at = slot * face
        pushed[slot][...] = dot(operator[at:at + face], push[...])


def image_kernel(nf, na, *refs):
    _, (operator, first), (image,) = split(refs, nf, na)
    image[...] = dot(operator[...], first[...])


def change_kernel(nf, na, *refs):
    (live,), (values, operator, shapes, first, image, own, coefs, *rest), (change, sums) = split(refs, nf, na)
    near, messages = rest[:4], rest[4:]
    face = values.shape[0] // SLOTS
    for slot, part in enumerate(corrected(live, values, shapes, own, coefs, near, messages)):
        change[slot * face:(slot + 1) * face] = part
    moved = dot(operator[...], change[...])

    def inner(left, right):
        return jnp.sum(left * right, axis=0, keepdims=True)

    sums[0:1] = inner(first[...], first[...])
    sums[1:2] = inner(first[...], image[...])
    sums[2:3] = inner(first[...], change[...])
    sums[3:4] = inner(change[...], change[...])
    sums[4:5] = inner(change[...], image[...])
    sums[5:6] = inner(change[...], moved)


def finish_kernel(nf, na, *refs):
    (contact,), (sums, first, push, change), (multipliers, direction) = split(refs, nf, na)
    face = first.shape[0] // SLOTS
    s = [sums[i:i + 1] for i in range(6)]
    step = s[0] / (2.0 * s[1])
    norm = s[0] + step * (2.0 * s[2] + step * s[3])
    curvature = 2.0 * (s[1] + step * (2.0 * s[4] + step * s[5]))
    ratio = norm / curvature
    for slot in range(SLOTS):
        rows = slice(slot * face, (slot + 1) * face)
        part = first[rows] + step * change[rows]
        direction[rows] = part
        multipliers[rows] = clamp(step * push[rows] - ratio * part, slot, contact[0, slot] > 0)


def opened(nf, na, *refs):
    (live,), (shapes, *faces), (values, spread) = split(refs, nf, na)
    pushed, gotten = faces[:SLOTS], faces[SLOTS:]
    face = values.shape[0] // SLOTS
    for slot in range(SLOTS):
        at = slot * face
        values[at:at + face] = live[0, slot].astype(jnp.float32) * (pushed[slot][...] - gotten[slot][...])
    coef = dot(shapes[...], values[...])
    for row in range(spread.shape[0]):
        spread[row] = coef


def body(dual_ops, gap_parts, modes, coarse_rows, face_live, contact):
    operator = dual_ops[0, 0]
    dual_rows = operator.shape[0]
    face = dual_rows // SLOTS
    cases = gap_parts.shape[3]
    kinds = modes.shape[3]
    groups = lax.axis_size("grp")
    live, touching = face_live[0], contact[0]
    rows = coarse_rows[0, 0]
    parts = gap_parts[0, 0]
    shapes = modes[0, 0].T
    short, long = face + kinds // 2, face + kinds // 2 + kinds
    whole = (dual_rows, cases)
    spread = (groups, kinds, cases)
    heavy = 12 * dual_rows * dual_rows * cases
    light = 12 * dual_rows * kinds * cases

    messages = kernel_call(
        pack_kernel, [], [parts, shapes, rows],
        [(short if slot < 4 else long, cases) for slot in range(SLOTS)], 0,
    )
    messages = exchange(messages)

    def coarse(spread_coef):
        coefs = swap(spread_coef, "grp").reshape(groups * kinds, cases)
        own, = kernel_call(coarse_kernel, [], [rows, coefs], [(kinds, cases)], light // 3)
        return own, coefs, exchange([own] * 4)

    values, coef = kernel_call(
        functools.partial(residual_kernel, -1.0), [live], [parts, shapes, *messages], [whole, spread], light
    )
    own, coefs, near = coarse(coef)
    first, push, *pushed = kernel_call(
        push_kernel, [live, touching], [values, operator, shapes, own, coefs, *near, *messages],
        [whole, whole] + [(face, cases)] * SLOTS, heavy + 2 * light,
    )
    gotten = exchange([pushed[slot ^ 1] for slot in range(SLOTS)])
    image, = kernel_call(image_kernel, [], [operator, first], [whole], heavy)
    values, coef = kernel_call(opened, [live], [shapes, *pushed, *gotten], [whole, spread], light)
    own, coefs, near = coarse(coef)
    change, sums = kernel_call(
        change_kernel, [live], [values, operator, shapes, first, image, own, coefs, *near, *messages],
        [whole, (6, cases)], heavy + 2 * light,
    )
    multipliers, direction = kernel_call(
        finish_kernel, [touching], [total(sums), first, push, change], [whole, whole], 8 * dual_rows * cases
    )
    shape = (1, 1) + whole
    return (multipliers.reshape(shape), direction.reshape(shape))


def solution(mesh):
    fine = Mesh(mesh.devices.reshape(4, 32, 2, 4), ("y", "z", "core", "grp"))
    wide = P(SUB, "grp", None, None)
    flags = P(SUB, "grp", None)
    return jax.shard_map(
        body, mesh=fine, in_specs=(wide, wide, wide, wide, flags, flags), out_specs=(wide, wide), check_vma=False
    )
```

```python
import functools
import math

import jax
import jax.numpy as jnp
from jax import lax
from jax.experimental import pallas as pl
from jax.experimental.pallas import tpu as pltpu
from jax.sharding import Mesh, PartitionSpec as P


SUBROW = 16
SLOTS = 6
LANES = 128
PLANE = ("y", "core", "grp")
SUB = ("y", "z", "core")
SOURCES = ((SUB, -1), (SUB, 1), (SUB, -SUBROW), (SUB, SUBROW), ("grp", -1), ("grp", 1))
ORDER = (2, 3, 0, 1, 4, 5)


def fetch(piece, slot):
    axis, offset = SOURCES[slot]
    count = lax.axis_size(axis)
    pairs = [(i, i - offset) for i in range(count) if 0 <= i - offset < count]
    return lax.ppermute(piece, axis, pairs)


def exchange(pieces):
    gotten = [None] * len(pieces)
    for slot in ORDER:
        if slot < len(pieces):
            gotten[slot] = fetch(pieces[slot], slot)
    return gotten


def swap(blocks, axes):
    return lax.all_to_all(blocks, axes, 0, 0, tiled=True)


def total(terms):
    plane = lax.axis_size(PLANE)
    chunks = terms.reshape(plane, -1)
    chunk = jnp.sum(swap(chunks, PLANE), axis=0)
    chunk = jnp.sum(swap(jnp.broadcast_to(chunk, (lax.axis_size("z"),) + chunk.shape), "z"), axis=0)
    return swap(jnp.broadcast_to(chunk, chunks.shape), PLANE).reshape(terms.shape)


def dot(left, right, across=1):
    return lax.dot_general(
        left, right, (((across,), (0,)), ((), ())),
        precision=lax.Precision.HIGHEST, preferred_element_type=jnp.float32,
    )


def clamp(values, slot, touching):
    bounded = jnp.maximum(values, 0.0) if slot % 2 else jnp.minimum(values, 0.0)
    return jnp.where(touching, bounded, values)


def kernel_call(body, flags, arrays, outs, flops):
    smem = pl.BlockSpec(memory_space=pltpu.SMEM)
    vmem = pl.BlockSpec(memory_space=pltpu.VMEM)
    moved = sum(a.size for a in arrays) + sum(math.prod(o) for o in outs)
    return pl.pallas_call(
        functools.partial(body, len(flags), len(arrays)),
        out_shape=[jax.ShapeDtypeStruct(o, jnp.float32) for o in outs],
        in_specs=[smem] * len(flags) + [vmem] * len(arrays),
        out_specs=[vmem] * len(outs),
        compiler_params=pltpu.CompilerParams(vmem_limit_bytes=24 << 20),
        cost_estimate=pl.CostEstimate(flops=flops, bytes_accessed=4 * moved, transcendentals=0),
    )(*flags, *arrays)


def split(refs, flags, arrays):
    return refs[:flags], refs[flags:flags + arrays], refs[flags + arrays:]


def pack_kernel(gap, shapes, rows, *refs):
    outs, (shapes_here, rows_here, sems) = refs[:SLOTS], refs[SLOTS:]
    face = gap.shape[0] // SLOTS
    half = shapes.shape[0] // 2
    copies = [
        pltpu.make_async_copy(shapes, shapes_here, sems.at[0]),
        pltpu.make_async_copy(rows, rows_here, sems.at[1]),
    ]
    for slot, out in enumerate(outs):
        piece = gap.at[pl.ds((slot ^ 1) * face, face)]
        copies.append(pltpu.make_async_copy(piece, out.at[pl.ds(0, face)], sems.at[2 + slot]))
    for copy in copies:
        copy.start()
    copies[0].wait()
    for slot, out in enumerate(outs):
        piece = shapes_here[:, (slot ^ 1) * face:(slot ^ 1) * face + face]
        out[face:face + half] = jnp.zeros((half, out.shape[1]), jnp.float32)
        out[face:face + half, :face] = piece[:half]
        out[face:face + half, LANES:LANES + face] = piece[half:]
    copies[1].wait()
    for out in outs[4:]:
        out[face + half:] = jnp.zeros((2 * half, out.shape[1]), jnp.float32)
        out[face + half:, :rows.shape[1]] = rows_here[...]
    for copy in copies[2:]:
        copy.wait()


def pack(gap, shapes, rows):
    face = gap.shape[0] // SLOTS
    short = face + shapes.shape[0] // 2
    heights = [short] * 4 + [short + shapes.shape[0]] * 2
    hbm = pl.BlockSpec(memory_space=pltpu.HBM)
    vmem = pl.BlockSpec(memory_space=pltpu.VMEM)
    return pl.pallas_call(
        pack_kernel,
        out_shape=[jax.ShapeDtypeStruct((height, gap.shape[1]), jnp.float32) for height in heights],
        in_specs=[hbm] * 3,
        out_specs=[vmem] * SLOTS,
        scratch_shapes=[
            pltpu.VMEM(shapes.shape, jnp.float32), pltpu.VMEM(rows.shape, jnp.float32),
            pltpu.SemaphoreType.DMA((2 + SLOTS,)),
        ],
        compiler_params=pltpu.CompilerParams(vmem_limit_bytes=67043328),
        name="pack",
    )(gap, shapes, rows)


def flags_kernel(nf, na, *refs):
    (live, contact), (gap, shapes), (flags, masked, kept) = split(refs, nf, na)
    face = gap.shape[0] // SLOTS
    for slot in range(SLOTS):
        shape = (1, flags.shape[1])
        rows = slice(slot * face, (slot + 1) * face)
        flags[slot:slot + 1] = jnp.full(shape, live[0, slot], jnp.int32).astype(jnp.float32)
        flags[8 + slot:9 + slot] = jnp.full(shape, contact[0, slot], jnp.int32).astype(jnp.float32)
        masked[rows] = flags[slot:slot + 1] * gap[rows]
    kept[...] = shapes[...]


def residual_kernel(nf, na, *refs):
    _, (flags, masked, shapes, *gotten), (values, spread) = split(refs, nf, na)
    face = values.shape[0] // SLOTS
    for slot in range(SLOTS):
        rows = slice(slot * face, (slot + 1) * face)
        values[rows] = flags[slot:slot + 1] * gotten[slot][:face] - masked[rows]
    coef = dot(shapes[...], values[...])
    for row in range(spread.shape[0]):
        spread[row] = coef


def opened_kernel(nf, na, *refs):
    _, (flags, shapes, *faces), (values, spread) = split(refs, nf, na)
    pushed, gotten = faces[:SLOTS], faces[SLOTS:]
    face = values.shape[0] // SLOTS
    for slot in range(SLOTS):
        rows = slice(slot * face, (slot + 1) * face)
        values[rows] = flags[slot:slot + 1] * (pushed[slot][...] - gotten[slot][...])
    coef = dot(shapes[...], values[...])
    for row in range(spread.shape[0]):
        spread[row] = coef


def coarse_kernel(nf, na, *refs):
    _, (rows, coefs), (own,) = split(refs, nf, na)
    own[...] = dot(rows[...], coefs[...])


def pairs_kernel(nf, na, *refs):
    (live,), (shapes, *messages), (pairs,) = split(refs, nf, na)
    face = pairs.shape[0] // SLOTS
    half = shapes.shape[0] // 2
    for slot in range(SLOTS):
        rows = slice(slot * face, (slot + 1) * face)
        packed = messages[slot][face:face + half]
        both = jnp.concatenate([shapes[:, rows], -packed[:, :face], -packed[:, LANES:LANES + face]])
        pairs[rows] = live[0, slot].astype(jnp.float32) * both.T


def beside_kernel(nf, na, *refs):
    _, (coefs, *messages), outs = split(refs, nf, na)
    for message, out in zip(messages, outs):
        out[...] = dot(message[message.shape[0] - out.shape[0]:, :coefs.shape[0]], coefs[...])


def corrected(values, pairs, own, near):
    face = values.shape[0] // SLOTS
    faces = []
    for slot in range(SLOTS):
        rows = slice(slot * face, (slot + 1) * face)
        faces.append(values[rows] - dot(pairs[rows], jnp.concatenate([own[...], near[slot][...]])))
    return faces


def push_kernel(nf, na, *refs):
    _, (flags, values, operator, pairs, own, *near), (first, push, *far) = split(refs, nf, na)
    face = values.shape[0] // SLOTS
    for slot, part in enumerate(corrected(values, pairs, own, near)):
        rows = slice(slot * face, (slot + 1) * face)
        first[rows] = part
        push[rows] = clamp(-part, slot, flags[8 + slot:9 + slot] > 0.0)
    image = dot(operator[2 * face:4 * face], push[...])
    for at, out in enumerate(far):
        out[...] = image[at * face:(at + 1) * face]


def rest_kernel(nf, na, *refs):
    _, (operator, push), outs = split(refs, nf, na)
    face = operator.shape[0] // SLOTS
    upper = dot(operator[:2 * face], push[...])
    lower = dot(operator[4 * face:], push[...])
    outs[0][...] = upper[:face]
    outs[1][...] = upper[face:]
    outs[2][...] = lower[:face]
    outs[3][...] = lower[face:]


def inner(left, right):
    return jnp.sum(left * right, axis=0, keepdims=True)


def image_kernel(nf, na, *refs):
    _, (operator, first), (image, sums) = split(refs, nf, na)
    image[...] = dot(operator[...], first[...])
    sums[0:1] = inner(first[...], first[...])
    sums[1:2] = inner(first[...], image[...])


def change_kernel(nf, na, *refs):
    _, (values, operator, pairs, first, image, early, own, *near), (change, sums) = split(refs, nf, na)
    face = values.shape[0] // SLOTS
    for slot, part in enumerate(corrected(values, pairs, own, near)):
        change[slot * face:(slot + 1) * face] = part
    moved = dot(operator[...], change[...])
    sums[0:2] = early[...]
    sums[2:3] = inner(first[...], change[...])
    sums[3:4] = inner(change[...], change[...])
    sums[4:5] = inner(change[...], image[...])
    sums[5:6] = inner(change[...], moved)


def finish_kernel(nf, na, *refs):
    _, (flags, sums, first, push, change), (multipliers, direction) = split(refs, nf, na)
    face = first.shape[0] // SLOTS
    s = [sums[i:i + 1] for i in range(6)]
    step = s[0] / (2.0 * s[1])
    norm = s[0] + step * (2.0 * s[2] + step * s[3])
    curvature = 2.0 * (s[1] + step * (2.0 * s[4] + step * s[5]))
    ratio = norm / curvature
    for slot in range(SLOTS):
        rows = slice(slot * face, (slot + 1) * face)
        part = first[rows] + step * change[rows]
        direction[rows] = part
        multipliers[rows] = clamp(step * push[rows] - ratio * part, slot, flags[8 + slot:9 + slot] > 0.0)


def body(dual_ops, gap_parts, modes, coarse_rows, face_live, contact):
    operator = dual_ops[0, 0]
    dual_rows = operator.shape[0]
    face = dual_rows // SLOTS
    cases = gap_parts.shape[3]
    kinds = modes.shape[3]
    groups = lax.axis_size("grp")
    live, touching = face_live[0], contact[0]
    rows = coarse_rows[0, 0]
    parts = gap_parts[0, 0]
    shapes = modes[0, 0].T
    whole = (dual_rows, cases)
    spread = (groups, kinds, cases)
    heavy = 12 * dual_rows * dual_rows * cases
    light = 12 * dual_rows * kinds * cases

    messages = exchange(pack(parts, shapes, rows))
    flags, masked, shapes = kernel_call(
        flags_kernel, [live, touching], [parts, shapes], [(16, cases), whole, shapes.shape], 0
    )

    def coarse(spread_coef):
        coefs = swap(spread_coef, "grp").reshape(groups * kinds, cases)
        own, = kernel_call(coarse_kernel, [], [rows, coefs], [(kinds, cases)], light // 3)
        near = exchange([own] * 4)
        beside = kernel_call(beside_kernel, [], [coefs, *messages[4:]], [(kinds, cases)] * 2, light)
        return [own, *near, *beside]

    values, coef = kernel_call(residual_kernel, [], [flags, masked, shapes, *messages], [whole, spread], light)
    known = coarse(coef)
    pairs, = kernel_call(pairs_kernel, [live], [shapes, *messages], [(dual_rows, 2 * kinds)], light)
    first, push, *far = kernel_call(
        push_kernel, [], [flags, values, operator, pairs, *known], [whole, whole] + [(face, cases)] * 2,
        heavy // 3 + 2 * light,
    )
    rest = kernel_call(rest_kernel, [], [operator, push], [(face, cases)] * 4, 2 * heavy // 3)
    pushed = [*rest[:2], *far, *rest[2:]]
    gotten = exchange([pushed[slot ^ 1] for slot in range(SLOTS)])
    image, early = kernel_call(image_kernel, [], [operator, first], [whole, (2, cases)], heavy)
    values, coef = kernel_call(opened_kernel, [], [flags, shapes, *pushed, *gotten], [whole, spread], light)
    known = coarse(coef)
    change, sums = kernel_call(
        change_kernel, [], [values, operator, pairs, first, image, early, *known],
        [whole, (6, cases)], heavy + 2 * light,
    )
    multipliers, direction = kernel_call(
        finish_kernel, [], [flags, total(sums), first, push, change], [whole, whole], 8 * dual_rows * cases
    )
    shape = (1, 1) + whole
    return (multipliers.reshape(shape), direction.reshape(shape))


def solution(mesh):
    fine = Mesh(mesh.devices.reshape(4, 32, 2, 4), ("y", "z", "core", "grp"))
    wide = P(SUB, "grp", None, None)
    flags = P(SUB, "grp", None)
    return jax.shard_map(
        body, mesh=fine, in_specs=(wide, wide, wide, wide, flags, flags), out_specs=(wide, wide), check_vma=False
    )
```

```python
import functools
import math

import jax
import jax.numpy as jnp
from jax import lax
from jax.experimental import pallas as pl
from jax.experimental.pallas import tpu as pltpu
from jax.sharding import Mesh, PartitionSpec as P


SUBROW = 16
SLOTS = 6
LANES = 128
CORE = 6
PLANE = ("y", "core", "grp")
SUB = ("y", "z", "core")
SOURCES = ((SUB, -1), (SUB, 1), (SUB, -SUBROW), (SUB, SUBROW), ("grp", -1), ("grp", 1))
ORDER = (2, 3, 1, 4, 5, 0)


def fetch(piece, slot):
    axis, offset = SOURCES[slot]
    count = lax.axis_size(axis)
    turned = [1 - 2 * (i % 2) if axis == SUB else 1 for i in range(count)]
    pairs = [(i, i - offset * turned[i]) for i in range(count) if 0 <= i - offset * turned[i] < count]
    return lax.ppermute(piece, axis, pairs)


def exchange(pieces):
    gotten = [None] * len(pieces)
    for slot in ORDER:
        if slot < len(pieces):
            gotten[slot] = fetch(pieces[slot], slot)
    return gotten


def swap(blocks, axes):
    return lax.all_to_all(blocks, axes, 0, 0, tiled=True)


def total(terms):
    plane = lax.axis_size(PLANE)
    chunks = terms.reshape(plane, -1)
    chunk = jnp.sum(swap(chunks, PLANE), axis=0)
    chunk = jnp.sum(swap(jnp.broadcast_to(chunk, (lax.axis_size("z"),) + chunk.shape), "z"), axis=0)
    return swap(jnp.broadcast_to(chunk, chunks.shape), PLANE)[:, None]


def dot(left, right, across=1):
    return lax.dot_general(
        left, right, (((across,), (0,)), ((), ())),
        precision=lax.Precision.HIGHEST, preferred_element_type=jnp.float32,
    )


def clamp(values, slot, touching):
    bounded = jnp.maximum(values, 0.0) if slot % 2 else jnp.minimum(values, 0.0)
    return jnp.where(touching, bounded, values)


def kernel_call(body, flags, arrays, outs, flops):
    smem = pl.BlockSpec(memory_space=pltpu.SMEM)
    vmem = pl.BlockSpec(memory_space=pltpu.VMEM)
    moved = sum(a.size for a in arrays) + sum(math.prod(o) for o in outs)
    return pl.pallas_call(
        functools.partial(body, len(flags), len(arrays)),
        out_shape=[jax.ShapeDtypeStruct(o, jnp.float32) for o in outs],
        in_specs=[smem] * len(flags) + [vmem] * len(arrays),
        out_specs=[vmem] * len(outs),
        compiler_params=pltpu.CompilerParams(vmem_limit_bytes=24 << 20),
        cost_estimate=pl.CostEstimate(flops=flops, bytes_accessed=4 * moved, transcendentals=0),
    )(*flags, *arrays)


def split(refs, flags, arrays):
    return refs[:flags], refs[flags:flags + arrays], refs[flags + arrays:]


def unturned(second, arrays, received):
    turned = []
    for lower, upper in ((0, 1), (2, 3)):
        low, up = arrays[lower], arrays[upper]
        if received and lower == 0:
            low, up = up, low
        turned.append(jnp.where(second, up, low))
        turned.append(jnp.where(second, low, up))
    return turned + list(arrays[4:])


def pack_kernel(gap, shapes, rows, *refs):
    outs, (shapes_here, rows_here, sems) = refs[:SLOTS], refs[SLOTS:]
    face = gap.shape[0] // SLOTS
    half = shapes.shape[0] // 2
    core = lax.axis_index("core")
    copies = [
        pltpu.make_async_copy(shapes, shapes_here, sems.at[0]),
        pltpu.make_async_copy(rows, rows_here, sems.at[1]),
    ]
    for slot, out in enumerate(outs):
        turn = 0 if slot >= 4 else core if slot % 2 else -core
        at = ((slot ^ 1) + turn) * face
        piece = gap.at[pl.ds(pl.multiple_of(at, 8), face)]
        copies.append(pltpu.make_async_copy(piece, out.at[pl.ds(0, face)], sems.at[2 + slot]))
    for copy in copies:
        copy.start()
    copies[0].wait()
    second = jnp.full((shapes.shape[0], face), core, jnp.int32) > 0
    pieces = [shapes_here[:, slot * face:(slot + 1) * face] for slot in range(SLOTS)]
    pieces = unturned(second, [pieces[slot ^ 1] for slot in range(SLOTS)], False)
    for piece, out in zip(pieces, outs):
        out[face:face + half] = jnp.zeros((half, out.shape[1]), jnp.float32)
        out[face:face + half, :face] = piece[:half]
        out[face:face + half, LANES:LANES + face] = piece[half:]
    copies[1].wait()
    for out in outs[4:]:
        out[face + half:] = jnp.zeros((2 * half, out.shape[1]), jnp.float32)
        out[face + half:, :rows.shape[1]] = rows_here[...]
    for copy in copies[2:]:
        copy.wait()


def pack(gap, shapes, rows):
    face = gap.shape[0] // SLOTS
    short = face + shapes.shape[0] // 2
    heights = [short] * 4 + [short + shapes.shape[0]] * 2
    hbm = pl.BlockSpec(memory_space=pltpu.HBM)
    vmem = pl.BlockSpec(memory_space=pltpu.VMEM)
    return pl.pallas_call(
        pack_kernel,
        out_shape=[jax.ShapeDtypeStruct((height, gap.shape[1]), jnp.float32) for height in heights],
        in_specs=[hbm] * 3,
        out_specs=[vmem] * SLOTS,
        scratch_shapes=[
            pltpu.VMEM(shapes.shape, jnp.float32), pltpu.VMEM(rows.shape, jnp.float32),
            pltpu.SemaphoreType.DMA((2 + SLOTS,)),
        ],
        compiler_params=pltpu.CompilerParams(vmem_limit_bytes=67043328),
        name="pack",
    )(gap, shapes, rows)


def flags_kernel(nf, na, *refs):
    (live, contact), (gap, shapes), (flags, masked, kept) = split(refs, nf, na)
    face = gap.shape[0] // SLOTS
    flags[CORE:CORE + 1] = jnp.full((1, flags.shape[1]), lax.axis_index("core"), jnp.int32).astype(jnp.float32)
    for slot in range(SLOTS):
        shape = (1, flags.shape[1])
        rows = slice(slot * face, (slot + 1) * face)
        flags[slot:slot + 1] = jnp.full(shape, live[0, slot], jnp.int32).astype(jnp.float32)
        flags[8 + slot:9 + slot] = jnp.full(shape, contact[0, slot], jnp.int32).astype(jnp.float32)
        masked[rows] = flags[slot:slot + 1] * gap[rows]
    kept[...] = shapes[...]


def residual_kernel(nf, na, *refs):
    _, (flags, masked, shapes, *messages), (values, spread) = split(refs, nf, na)
    face = values.shape[0] // SLOTS
    gotten = unturned(flags[CORE:CORE + 1] > 0.0, [message[:face] for message in messages], True)
    for slot in range(SLOTS):
        rows = slice(slot * face, (slot + 1) * face)
        values[rows] = flags[slot:slot + 1] * gotten[slot] - masked[rows]
    coef = dot(shapes[...], values[...])
    for row in range(spread.shape[0]):
        spread[row] = coef


def opened_kernel(nf, na, *refs):
    _, (flags, shapes, *faces), (values, spread) = split(refs, nf, na)
    second = flags[CORE:CORE + 1] > 0.0
    gotten = unturned(second, [array[...] for array in faces[SLOTS:]], True)
    sent = unturned(second, [array[...] for array in faces[:SLOTS]], False)
    face = values.shape[0] // SLOTS
    for slot in range(SLOTS):
        rows = slice(slot * face, (slot + 1) * face)
        values[rows] = flags[slot:slot + 1] * (sent[slot ^ 1] - gotten[slot])
    coef = dot(shapes[...], values[...])
    for row in range(spread.shape[0]):
        spread[row] = coef


def coarse_kernel(nf, na, *refs):
    _, (rows, coefs), (own,) = split(refs, nf, na)
    own[...] = dot(rows[...], coefs[...])


def pairs_kernel(nf, na, *refs):
    (live,), (flags, shapes, *messages), (pairs,) = split(refs, nf, na)
    face = pairs.shape[0] // SLOTS
    half = shapes.shape[0] // 2
    packs = unturned(flags[CORE:CORE + 1] > 0.0, [message[face:face + half] for message in messages], True)
    for slot in range(SLOTS):
        rows = slice(slot * face, (slot + 1) * face)
        packed = packs[slot]
        both = jnp.concatenate([shapes[:, rows], -packed[:, :face], -packed[:, LANES:LANES + face]])
        pairs[rows] = live[0, slot].astype(jnp.float32) * both.T


def beside_kernel(nf, na, *refs):
    _, (coefs, *messages), outs = split(refs, nf, na)
    for message, out in zip(messages, outs):
        out[...] = dot(message[message.shape[0] - out.shape[0]:, :coefs.shape[0]], coefs[...])


def corrected(flags, values, pairs, own, near):
    face = values.shape[0] // SLOTS
    near = unturned(flags[CORE:CORE + 1] > 0.0, [array[...] for array in near], True)
    faces = []
    for slot in range(SLOTS):
        rows = slice(slot * face, (slot + 1) * face)
        faces.append(values[rows] - dot(pairs[rows], jnp.concatenate([own[...], near[slot]])))
    return faces


def push_kernel(nf, na, *refs):
    _, (flags, values, operator, pairs, own, *near), (first, push, *far) = split(refs, nf, na)
    face = values.shape[0] // SLOTS
    for slot, part in enumerate(corrected(flags, values, pairs, own, near)):
        rows = slice(slot * face, (slot + 1) * face)
        first[rows] = part
        push[rows] = clamp(-part, slot, flags[8 + slot:9 + slot] > 0.0)
    image = dot(operator[2 * face:4 * face], push[...])
    second = flags[CORE:CORE + 1] > 0.0
    lower, upper = image[:face], image[face:]
    far[0][...] = jnp.where(second, lower, upper)
    far[1][...] = jnp.where(second, upper, lower)


def rest_kernel(nf, na, *refs):
    _, (flags, operator, push), outs = split(refs, nf, na)
    second = flags[CORE:CORE + 1] > 0.0
    face = operator.shape[0] // SLOTS
    upper = dot(operator[:2 * face], push[...])
    lower = dot(operator[4 * face:], push[...])
    outs[0][...] = jnp.where(second, upper[:face], upper[face:])
    outs[1][...] = jnp.where(second, upper[face:], upper[:face])
    outs[2][...] = lower[face:]
    outs[3][...] = lower[:face]


def inner(left, right):
    return jnp.sum(left * right, axis=0, keepdims=True)


def image_kernel(nf, na, *refs):
    _, (operator, first), (image, sums) = split(refs, nf, na)
    image[...] = dot(operator[...], first[...])
    sums[0:1] = inner(first[...], first[...])
    sums[1:2] = inner(first[...], image[...])


def change_kernel(nf, na, *refs):
    _, (flags, values, operator, pairs, first, image, early, own, *near), (change, sums) = split(refs, nf, na)
    face = values.shape[0] // SLOTS
    for slot, part in enumerate(corrected(flags, values, pairs, own, near)):
        change[slot * face:(slot + 1) * face] = part
    moved = dot(operator[...], change[...])
    sums[0:2] = early[...]
    sums[2:3] = inner(first[...], change[...])
    sums[3:4] = inner(change[...], change[...])
    sums[4:5] = inner(change[...], image[...])
    sums[5:6] = inner(change[...], moved)


def finish_kernel(nf, na, *refs):
    _, (flags, sums, first, push, change), (multipliers, direction) = split(refs, nf, na)
    face = first.shape[0] // SLOTS
    flat = jnp.concatenate([sums[i] for i in range(sums.shape[0])], axis=1)
    cases = first.shape[1]
    s = [flat[:, i * cases:(i + 1) * cases] for i in range(6)]
    step = s[0] / (2.0 * s[1])
    norm = s[0] + step * (2.0 * s[2] + step * s[3])
    curvature = 2.0 * (s[1] + step * (2.0 * s[4] + step * s[5]))
    ratio = norm / curvature
    for slot in range(SLOTS):
        rows = slice(slot * face, (slot + 1) * face)
        part = first[rows] + step * change[rows]
        direction[rows] = part
        multipliers[rows] = clamp(step * push[rows] - ratio * part, slot, flags[8 + slot:9 + slot] > 0.0)


def body(dual_ops, gap_parts, modes, coarse_rows, face_live, contact):
    operator = dual_ops[0, 0]
    dual_rows = operator.shape[0]
    face = dual_rows // SLOTS
    cases = gap_parts.shape[3]
    kinds = modes.shape[3]
    groups = lax.axis_size("grp")
    live, touching = face_live[0], contact[0]
    rows = coarse_rows[0, 0]
    parts = gap_parts[0, 0]
    shapes = modes[0, 0].T
    whole = (dual_rows, cases)
    spread = (groups, kinds, cases)
    heavy = 12 * dual_rows * dual_rows * cases
    light = 12 * dual_rows * kinds * cases

    messages = exchange(pack(parts, shapes, rows))
    flags, masked, shapes = kernel_call(
        flags_kernel, [live, touching], [parts, shapes], [(16, cases), whole, shapes.shape], 0
    )

    def coarse(spread_coef):
        coefs = swap(spread_coef, "grp").reshape(groups * kinds, cases)
        own, = kernel_call(coarse_kernel, [], [rows, coefs], [(kinds, cases)], light // 3)
        near = exchange([own] * 4)
        beside = kernel_call(beside_kernel, [], [coefs, *messages[4:]], [(kinds, cases)] * 2, light)
        return [own, *near, *beside]

    values, coef = kernel_call(residual_kernel, [], [flags, masked, shapes, *messages], [whole, spread], light)
    known = coarse(coef)
    pairs, = kernel_call(pairs_kernel, [live], [flags, shapes, *messages], [(dual_rows, 2 * kinds)], light)
    first, push, *far = kernel_call(
        push_kernel, [], [flags, values, operator, pairs, *known], [whole, whole] + [(face, cases)] * 2,
        heavy // 3 + 2 * light,
    )
    rest = kernel_call(rest_kernel, [], [flags, operator, push], [(face, cases)] * 4, 2 * heavy // 3)
    sent = [*rest[:2], *far, *rest[2:]]
    gotten = exchange(sent)
    image, early = kernel_call(image_kernel, [], [operator, first], [whole, (2, cases)], heavy)
    values, coef = kernel_call(opened_kernel, [], [flags, shapes, *sent, *gotten], [whole, spread], light)
    known = coarse(coef)
    change, sums = kernel_call(
        change_kernel, [], [flags, values, operator, pairs, first, image, early, *known],
        [whole, (6, cases)], heavy + 2 * light,
    )
    multipliers, direction = kernel_call(
        finish_kernel, [], [flags, total(sums), first, push, change], [whole, whole], 8 * dual_rows * cases
    )
    shape = (1, 1) + whole
    return (multipliers.reshape(shape), direction.reshape(shape))


def solution(mesh):
    fine = Mesh(mesh.devices.reshape(4, 32, 2, 4), ("y", "z", "core", "grp"))
    wide = P(SUB, "grp", None, None)
    flags = P(SUB, "grp", None)
    return jax.shard_map(
        body, mesh=fine, in_specs=(wide, wide, wide, wide, flags, flags), out_specs=(wide, wide), check_vma=False
    )
```

```python
import functools
import math

import jax
import jax.numpy as jnp
from jax import lax
from jax.experimental import pallas as pl
from jax.experimental.pallas import tpu as pltpu
from jax.sharding import Mesh, PartitionSpec as P


SUBROW = 16
SLOTS = 6
LANES = 128
CORE = 6
PLANE = ("y", "core", "grp")
SUB = ("y", "z", "core")
GRP = ("core", "grp")
SOURCES = ((SUB, -1), (SUB, 1), (SUB, -SUBROW), (SUB, SUBROW), (GRP, -1), (GRP, 1))
ORDER = (2, 3, 1, 4, 5, 0)


def fetch(piece, slot):
    axis, offset = SOURCES[slot]
    count = lax.axis_size(axis)
    span = lax.axis_size("grp") if axis == GRP else count
    pairs = []
    for i in range(count):
        core = i // span if axis == GRP else i % 2
        at = i % span - offset * (1 - 2 * core)
        if 0 <= at < span:
            pairs.append((i, i - i % span + at))
    return lax.ppermute(piece, axis, pairs)


def exchange(pieces):
    gotten = [None] * len(pieces)
    for slot in ORDER:
        if slot < len(pieces):
            gotten[slot] = fetch(pieces[slot], slot)
    return gotten


def swap(blocks, axes):
    return lax.all_to_all(blocks, axes, 0, 0, tiled=True)


def total(terms):
    plane = lax.axis_size(PLANE)
    chunks = terms.reshape(plane, -1)
    chunk = jnp.sum(swap(chunks, PLANE), axis=0)
    chunk = jnp.sum(swap(jnp.broadcast_to(chunk, (lax.axis_size("z"),) + chunk.shape), "z"), axis=0)
    return swap(jnp.broadcast_to(chunk, chunks.shape), PLANE)[:, None]


def dot(left, right, across=1):
    return lax.dot_general(
        left, right, (((across,), (0,)), ((), ())),
        precision=lax.Precision.HIGHEST, preferred_element_type=jnp.float32,
    )


def clamp(values, slot, touching):
    bounded = jnp.maximum(values, 0.0) if slot % 2 else jnp.minimum(values, 0.0)
    return jnp.where(touching, bounded, values)


def kernel_call(body, flags, arrays, outs, flops):
    smem = pl.BlockSpec(memory_space=pltpu.SMEM)
    vmem = pl.BlockSpec(memory_space=pltpu.VMEM)
    moved = sum(a.size for a in arrays) + sum(math.prod(o) for o in outs)
    return pl.pallas_call(
        functools.partial(body, len(flags), len(arrays)),
        out_shape=[jax.ShapeDtypeStruct(o, jnp.float32) for o in outs],
        in_specs=[smem] * len(flags) + [vmem] * len(arrays),
        out_specs=[vmem] * len(outs),
        compiler_params=pltpu.CompilerParams(vmem_limit_bytes=24 << 20),
        cost_estimate=pl.CostEstimate(flops=flops, bytes_accessed=4 * moved, transcendentals=0),
    )(*flags, *arrays)


def split(refs, flags, arrays):
    return refs[:flags], refs[flags:flags + arrays], refs[flags + arrays:]


def unturned(second, arrays, received):
    turned = []
    for lower, upper in ((0, 1), (2, 3), (4, 5)):
        low, up = arrays[lower], arrays[upper]
        if received and lower == 0:
            low, up = up, low
        turned.append(jnp.where(second, up, low))
        turned.append(jnp.where(second, low, up))
    return turned


def pack_kernel(gap, shapes, rows, *refs):
    outs, (shapes_here, rows_here, sems) = refs[:SLOTS], refs[SLOTS:]
    face = gap.shape[0] // SLOTS
    half = shapes.shape[0] // 2
    core = lax.axis_index("core")
    copies = [
        pltpu.make_async_copy(shapes, shapes_here, sems.at[0]),
        pltpu.make_async_copy(rows, rows_here, sems.at[1]),
    ]
    for slot, out in enumerate(outs):
        turn = core if slot % 2 else -core
        at = ((slot ^ 1) + turn) * face
        piece = gap.at[pl.ds(pl.multiple_of(at, 8), face)]
        copies.append(pltpu.make_async_copy(piece, out.at[pl.ds(0, face)], sems.at[2 + slot]))
    for copy in copies:
        copy.start()
    copies[0].wait()
    second = jnp.full((shapes.shape[0], face), core, jnp.int32) > 0
    pieces = [shapes_here[:, slot * face:(slot + 1) * face] for slot in range(SLOTS)]
    pieces = unturned(second, [pieces[slot ^ 1] for slot in range(SLOTS)], False)
    for piece, out in zip(pieces, outs):
        out[face:face + half] = jnp.zeros((half, out.shape[1]), jnp.float32)
        out[face:face + half, :face] = piece[:half]
        out[face:face + half, LANES:LANES + face] = piece[half:]
    copies[1].wait()
    for out in outs[4:]:
        out[face + half:] = jnp.zeros((2 * half, out.shape[1]), jnp.float32)
        out[face + half:, :rows.shape[1]] = rows_here[...]
    for copy in copies[2:]:
        copy.wait()


def pack(gap, shapes, rows):
    face = gap.shape[0] // SLOTS
    short = face + shapes.shape[0] // 2
    heights = [short] * 4 + [short + shapes.shape[0]] * 2
    hbm = pl.BlockSpec(memory_space=pltpu.HBM)
    vmem = pl.BlockSpec(memory_space=pltpu.VMEM)
    return pl.pallas_call(
        pack_kernel,
        out_shape=[jax.ShapeDtypeStruct((height, gap.shape[1]), jnp.float32) for height in heights],
        in_specs=[hbm] * 3,
        out_specs=[vmem] * SLOTS,
        scratch_shapes=[
            pltpu.VMEM(shapes.shape, jnp.float32), pltpu.VMEM(rows.shape, jnp.float32),
            pltpu.SemaphoreType.DMA((2 + SLOTS,)),
        ],
        compiler_params=pltpu.CompilerParams(vmem_limit_bytes=67043328),
        name="pack",
    )(gap, shapes, rows)


def flags_kernel(nf, na, *refs):
    (live, contact), (gap, shapes), (flags, masked, kept) = split(refs, nf, na)
    face = gap.shape[0] // SLOTS
    flags[CORE:CORE + 1] = jnp.full((1, flags.shape[1]), lax.axis_index("core"), jnp.int32).astype(jnp.float32)
    for slot in range(SLOTS):
        shape = (1, flags.shape[1])
        rows = slice(slot * face, (slot + 1) * face)
        flags[slot:slot + 1] = jnp.full(shape, live[0, slot], jnp.int32).astype(jnp.float32)
        flags[8 + slot:9 + slot] = jnp.full(shape, contact[0, slot], jnp.int32).astype(jnp.float32)
        masked[rows] = flags[slot:slot + 1] * gap[rows]
    kept[...] = shapes[...]


def residual_kernel(nf, na, *refs):
    _, (flags, masked, shapes, *messages), (values, spread) = split(refs, nf, na)
    face = values.shape[0] // SLOTS
    gotten = unturned(flags[CORE:CORE + 1] > 0.0, [message[:face] for message in messages], True)
    for slot in range(SLOTS):
        rows = slice(slot * face, (slot + 1) * face)
        values[rows] = flags[slot:slot + 1] * gotten[slot] - masked[rows]
    coef = dot(shapes[...], values[...])
    for row in range(spread.shape[0]):
        spread[row] = coef


def opened_kernel(nf, na, *refs):
    _, (flags, shapes, *faces), (values, spread) = split(refs, nf, na)
    second = flags[CORE:CORE + 1] > 0.0
    gotten = unturned(second, [array[...] for array in faces[SLOTS:]], True)
    sent = unturned(second, [array[...] for array in faces[:SLOTS]], False)
    face = values.shape[0] // SLOTS
    for slot in range(SLOTS):
        rows = slice(slot * face, (slot + 1) * face)
        values[rows] = flags[slot:slot + 1] * (sent[slot ^ 1] - gotten[slot])
    coef = dot(shapes[...], values[...])
    for row in range(spread.shape[0]):
        spread[row] = coef


def coarse_kernel(nf, na, *refs):
    _, (rows, coefs), (own,) = split(refs, nf, na)
    own[...] = dot(rows[...], coefs[...])


def pairs_kernel(nf, na, *refs):
    (live,), (flags, shapes, *messages), (pairs,) = split(refs, nf, na)
    face = pairs.shape[0] // SLOTS
    half = shapes.shape[0] // 2
    packs = unturned(flags[CORE:CORE + 1] > 0.0, [message[face:face + half] for message in messages], True)
    for slot in range(SLOTS):
        rows = slice(slot * face, (slot + 1) * face)
        packed = packs[slot]
        both = jnp.concatenate([shapes[:, rows], -packed[:, :face], -packed[:, LANES:LANES + face]])
        pairs[rows] = live[0, slot].astype(jnp.float32) * both.T


def beside_kernel(nf, na, *refs):
    _, (coefs, *messages), outs = split(refs, nf, na)
    for message, out in zip(messages, outs):
        out[...] = dot(message[message.shape[0] - out.shape[0]:, :coefs.shape[0]], coefs[...])


def corrected(flags, values, pairs, own, near):
    face = values.shape[0] // SLOTS
    near = unturned(flags[CORE:CORE + 1] > 0.0, [array[...] for array in near], True)
    faces = []
    for slot in range(SLOTS):
        rows = slice(slot * face, (slot + 1) * face)
        faces.append(values[rows] - dot(pairs[rows], jnp.concatenate([own[...], near[slot]])))
    return faces


def push_kernel(nf, na, *refs):
    _, (flags, values, operator, pairs, own, *near), (first, push, *far) = split(refs, nf, na)
    face = values.shape[0] // SLOTS
    for slot, part in enumerate(corrected(flags, values, pairs, own, near)):
        rows = slice(slot * face, (slot + 1) * face)
        first[rows] = part
        push[rows] = clamp(-part, slot, flags[8 + slot:9 + slot] > 0.0)
    image = dot(operator[2 * face:4 * face], push[...])
    second = flags[CORE:CORE + 1] > 0.0
    lower, upper = image[:face], image[face:]
    far[0][...] = jnp.where(second, lower, upper)
    far[1][...] = jnp.where(second, upper, lower)


def rest_kernel(nf, na, *refs):
    _, (flags, operator, push), outs = split(refs, nf, na)
    second = flags[CORE:CORE + 1] > 0.0
    face = operator.shape[0] // SLOTS
    upper = dot(operator[:2 * face], push[...])
    lower = dot(operator[4 * face:], push[...])
    outs[0][...] = jnp.where(second, upper[:face], upper[face:])
    outs[1][...] = jnp.where(second, upper[face:], upper[:face])
    outs[2][...] = jnp.where(second, lower[:face], lower[face:])
    outs[3][...] = jnp.where(second, lower[face:], lower[:face])


def inner(left, right):
    return jnp.sum(left * right, axis=0, keepdims=True)


def image_kernel(nf, na, *refs):
    _, (operator, first), (image, sums) = split(refs, nf, na)
    image[...] = dot(operator[...], first[...])
    sums[0:1] = inner(first[...], first[...])
    sums[1:2] = inner(first[...], image[...])


def change_kernel(nf, na, *refs):
    _, (flags, values, operator, pairs, first, image, early, own, *near), (change, sums) = split(refs, nf, na)
    face = values.shape[0] // SLOTS
    for slot, part in enumerate(corrected(flags, values, pairs, own, near)):
        change[slot * face:(slot + 1) * face] = part
    moved = dot(operator[...], change[...])
    sums[0:2] = early[...]
    sums[2:3] = inner(first[...], change[...])
    sums[3:4] = inner(change[...], change[...])
    sums[4:5] = inner(change[...], image[...])
    sums[5:6] = inner(change[...], moved)


def finish_kernel(nf, na, *refs):
    _, (flags, sums, first, push, change), (multipliers, direction) = split(refs, nf, na)
    face = first.shape[0] // SLOTS
    flat = jnp.concatenate([sums[i] for i in range(sums.shape[0])], axis=1)
    cases = first.shape[1]
    s = [flat[:, i * cases:(i + 1) * cases] for i in range(6)]
    step = s[0] / (2.0 * s[1])
    norm = s[0] + step * (2.0 * s[2] + step * s[3])
    curvature = 2.0 * (s[1] + step * (2.0 * s[4] + step * s[5]))
    ratio = norm / curvature
    for slot in range(SLOTS):
        rows = slice(slot * face, (slot + 1) * face)
        part = first[rows] + step * change[rows]
        direction[rows] = part
        multipliers[rows] = clamp(step * push[rows] - ratio * part, slot, flags[8 + slot:9 + slot] > 0.0)


def body(dual_ops, gap_parts, modes, coarse_rows, face_live, contact):
    operator = dual_ops[0, 0]
    dual_rows = operator.shape[0]
    face = dual_rows // SLOTS
    cases = gap_parts.shape[3]
    kinds = modes.shape[3]
    groups = lax.axis_size("grp")
    live, touching = face_live[0], contact[0]
    rows = coarse_rows[0, 0]
    parts = gap_parts[0, 0]
    shapes = modes[0, 0].T
    whole = (dual_rows, cases)
    spread = (groups, kinds, cases)
    heavy = 12 * dual_rows * dual_rows * cases
    light = 12 * dual_rows * kinds * cases

    messages = exchange(pack(parts, shapes, rows))
    flags, masked, shapes = kernel_call(
        flags_kernel, [live, touching], [parts, shapes], [(16, cases), whole, shapes.shape], 0
    )

    def coarse(spread_coef):
        coefs = swap(spread_coef, "grp").reshape(groups * kinds, cases)
        own, = kernel_call(coarse_kernel, [], [rows, coefs], [(kinds, cases)], light // 3)
        near = exchange([own] * 4)
        beside = kernel_call(beside_kernel, [], [coefs, *messages[4:]], [(kinds, cases)] * 2, light)
        return [own, *near, *beside]

    values, coef = kernel_call(residual_kernel, [], [flags, masked, shapes, *messages], [whole, spread], light)
    known = coarse(coef)
    pairs, = kernel_call(pairs_kernel, [live], [flags, shapes, *messages], [(dual_rows, 2 * kinds)], light)
    first, push, *far = kernel_call(
        push_kernel, [], [flags, values, operator, pairs, *known], [whole, whole] + [(face, cases)] * 2,
        heavy // 3 + 2 * light,
    )
    rest = kernel_call(rest_kernel, [], [flags, operator, push], [(face, cases)] * 4, 2 * heavy // 3)
    sent = [*rest[:2], *far, *rest[2:]]
    gotten = exchange(sent)
    image, early = kernel_call(image_kernel, [], [operator, first], [whole, (2, cases)], heavy)
    values, coef = kernel_call(opened_kernel, [], [flags, shapes, *sent, *gotten], [whole, spread], light)
    known = coarse(coef)
    change, sums = kernel_call(
        change_kernel, [], [flags, values, operator, pairs, first, image, early, *known],
        [whole, (6, cases)], heavy + 2 * light,
    )
    multipliers, direction = kernel_call(
        finish_kernel, [], [flags, total(sums), first, push, change], [whole, whole], 8 * dual_rows * cases
    )
    shape = (1, 1) + whole
    return (multipliers.reshape(shape), direction.reshape(shape))


def solution(mesh):
    fine = Mesh(mesh.devices.reshape(4, 32, 2, 4), ("y", "z", "core", "grp"))
    wide = P(SUB, "grp", None, None)
    flags = P(SUB, "grp", None)
    return jax.shard_map(
        body, mesh=fine, in_specs=(wide, wide, wide, wide, flags, flags), out_specs=(wide, wide), check_vma=False
    )
```
